32 devices in a mesh: dp: 16 (over z, x, core), group: 2 (over y).
Axes of the slice: x: 2, y: 2, z: 4, core: 2. Of those that a mesh axis runs over, the one named last changes fastest.
Arguments:
- hidden_in: bfloat16 [4096, 768], P(('dp', 'group')), may hold values from -6 to 6
- out_grad: bfloat16 [4096, 768], P(('dp', 'group')), may hold values from -6 to 6
- joint_weight: float32 [768, 2304], P('group', 'dp'), may hold values from -4 to 4
- mixer_weight: float32 [768, 768], P('group', 'dp'), may hold values from -4 to 4
- expand_weight: float32 [768, 2304], P('group', 'dp'), may hold values from -0.21875 to 0.21875
- reduce_weight: float32 [1152, 768], P('group', 'dp'), may hold values from -0.1875 to 0.1875
- mixer_gain: float32 [768], P('dp'), may hold values from 0.5 to 1.5
- expand_gain: float32 [768], P('dp'), may hold values from 0.5 to 1.5
- joint_first: float32 [768, 2304], P('group', 'dp'), may hold values from -0.0008544922 to 0.0008544922
- mixer_first: float32 [768, 768], P('group', 'dp'), may hold values from -0.0008544922 to 0.0008544922
- expand_first: float32 [768, 2304], P('group', 'dp'), may hold values from -0.0008544922 to 0.0008544922
- reduce_first: float32 [1152, 768], P('group', 'dp'), may hold values from -0.0008544922 to 0.0008544922
- mixer_gain_first: float32 [768], P('dp'), may hold values from -0.0008544922 to 0.0008544922
- expand_gain_first: float32 [768], P('dp'), may hold values from -0.0008544922 to 0.0008544922
- joint_second: float32 [768, 2304], P('group', 'dp'), may hold values from 3.988004e-11 to 3.988004e-10
- mixer_second: float32 [768, 768], P('group', 'dp'), may hold values from 3.988004e-11 to 3.988004e-10
- expand_second: float32 [768, 2304], P('group', 'dp'), may hold values from 3.988004e-11 to 3.988004e-10
- reduce_second: float32 [1152, 768], P('group', 'dp'), may hold values from 3.988004e-11 to 3.988004e-10
- mixer_gain_second: float32 [768], P('dp'), may hold values from 3.988004e-11 to 3.988004e-10
- expand_gain_second: float32 [768], P('dp'), may hold values from 3.988004e-11 to 3.988004e-10
Outputs:
- block_output: bfloat16 [4096, 768], P(('dp', 'group'))
- input_grad: float32 [4096, 768], P(('dp', 'group'))
- joint_grad: float32 [768, 2304], P('group', 'dp')
- mixer_grad: float32 [768, 768], P('group', 'dp')
- expand_grad: float32 [768, 2304], P('group', 'dp')
- reduce_grad: float32 [1152, 768], P('group', 'dp')
- mixer_gain_grad: float32 [768], P('dp')
- expand_gain_grad: float32 [768], P('dp')
- joint_new: float32 [768, 2304], P('group', 'dp')
- mixer_new: float32 [768, 768], P('group', 'dp')
- expand_new: float32 [768, 2304], P('group', 'dp')
- reduce_new: float32 [1152, 768], P('group', 'dp')
- mixer_gain_new: float32 [768], P('dp')
- expand_gain_new: float32 [768], P('dp')
- joint_first_new: float32 [768, 2304], P('group', 'dp')
- mixer_first_new: float32 [768, 768], P('group', 'dp')
- expand_first_new: float32 [768, 2304], P('group', 'dp')
- reduce_first_new: float32 [1152, 768], P('group', 'dp')
- mixer_gain_first_new: float32 [768], P('dp')
- expand_gain_first_new: float32 [768], P('dp')
- joint_second_new: float32 [768, 2304], P('group', 'dp')
- mixer_second_new: float32 [768, 768], P('group', 'dp')
- expand_second_new: float32 [768, 2304], P('group', 'dp')
- reduce_second_new: float32 [1152, 768], P('group', 'dp')
- mixer_gain_second_new: float32 [768], P('dp')
- expand_gain_second_new: float32 [768], P('dp')
The draws below stay inside these ranges and needn't reach their ends.
All inputs are finite; a program needn't handle non-finite values.
Results may differ from the reference program's by a relative error of at most 0.02.
Values may be sent and summed in bfloat16 or wider, within the bound.
No kernel may reach another device: no remote copies, remote signals or barrier semaphores. Data moves between devices by JAX's collectives and lax.ppermute only.
A program may use at most 128 MiB of HBM per device.

```python
import math
import jax
import jax.numpy as jnp
from jax import lax

D = 768
HEADS = 12
FF = 1152
HEAD_DIM = 64
SEQ = 256
TOKENS = 4096
N_DP = 16


def draw_joint_weight(key, part):
    base = jax.random.truncated_normal(key, -4.0, 4.0, (D, 3 * D), jnp.float32) / math.sqrt(D)
    return base


def steps_of(stream_key, dims, cuts, smallest, top_value):
    gain = 1.0
    for position, shards_of in cuts:
        steps = jax.random.uniform(jax.random.fold_in(jax.random.fold_in(stream_key, 6), position), (shards_of,), jnp.float32, smallest / len(cuts), top_value / len(cuts))
        gain = gain * jnp.repeat(jnp.exp(steps), dims[position] // shards_of).reshape((-1,) + (1,) * (len(dims) - 1 - position))
    return gain


def gaussian(key, extent, width, bound, cuts=(), kind=jnp.bfloat16):
    loudness = steps_of(key, extent, cuts, -0.22, 0.18) if cuts else 1.0
    result = jax.random.normal(key, extent, jnp.float32) * width * loudness
    return jnp.minimum(jnp.maximum(result, -bound), bound).astype(kind)


def setup_inputs(seed: int = 0) -> dict:
    key_of = jax.random.split(jax.random.key(seed), 21)
    return {
        "hidden_in": gaussian(key_of[0], (TOKENS, D), 1.0, 6.0, ((0, 32),)),
        "out_grad": gaussian(key_of[1], (TOKENS, D), 1.0, 6.0, ((0, 32),)),
        "joint_weight": draw_joint_weight(jax.random.fold_in(key_of[20], 71), 0),
        "mixer_weight": gaussian(key_of[3], (D, D), 2 ** -0.5, 4.0, ((0, 2), (1, 16)), jnp.float32),
        "expand_weight": gaussian(key_of[4], (D, 2 * FF), D ** -0.5, 0.21875, ((0, 2), (1, 16)), jnp.float32),
        "reduce_weight": gaussian(key_of[5], (FF, D), FF ** -0.5, 0.1875, ((0, 2), (1, 16)), jnp.float32),
        "mixer_gain": jnp.clip(1.0 + 0.1 * jax.random.normal(key_of[6], (D,), jnp.float32), 0.5, 1.5),
        "expand_gain": jnp.clip(1.0 + 0.1 * jax.random.normal(key_of[7], (D,), jnp.float32), 0.5, 1.5),
        "joint_first": gaussian(key_of[8], (D, 3 * D), (0.3 * (4 * D * D + 3 * D * FF + 2 * D) ** -0.5), 0.0008544922, ((0, 2), (1, 16)), jnp.float32),
        "mixer_first": gaussian(key_of[9], (D, D), (0.3 * (4 * D * D + 3 * D * FF + 2 * D) ** -0.5), 0.0008544922, ((0, 2), (1, 16)), jnp.float32),
        "expand_first": gaussian(key_of[10], (D, 2 * FF), (0.3 * (4 * D * D + 3 * D * FF + 2 * D) ** -0.5), 0.0008544922, ((0, 2), (1, 16)), jnp.float32),
        "reduce_first": gaussian(key_of[11], (FF, D), (0.3 * (4 * D * D + 3 * D * FF + 2 * D) ** -0.5), 0.0008544922, ((0, 2), (1, 16)), jnp.float32),
        "mixer_gain_first": gaussian(key_of[12], (D,), (0.3 * (4 * D * D + 3 * D * FF + 2 * D) ** -0.5), 0.0008544922, ((0, 16),), jnp.float32),
        "expand_gain_first": gaussian(key_of[13], (D,), (0.3 * (4 * D * D + 3 * D * FF + 2 * D) ** -0.5), 0.0008544922, ((0, 16),), jnp.float32),
        "joint_second": jnp.clip(jnp.exp(math.log(3.988004093624653e-10) - 2.3025851 * jax.random.uniform(key_of[14], (D, 3 * D), jnp.float32) ** steps_of(key_of[14], (D, 3 * D), ((0, 2), (1, 16)), -0.2, 0.2)), 3.988004024235714e-11, 3.988004093624653e-10),
        "mixer_second": jnp.clip(jnp.exp(math.log(3.988004093624653e-10) - 2.3025851 * jax.random.uniform(key_of[15], (D, D), jnp.float32) ** steps_of(key_of[15], (D, D), ((0, 2), (1, 16)), -0.2, 0.2)), 3.988004024235714e-11, 3.988004093624653e-10),
        "expand_second": jnp.clip(jnp.exp(math.log(3.988004093624653e-10) - 2.3025851 * jax.random.uniform(key_of[16], (D, 2 * FF), jnp.float32) ** steps_of(key_of[16], (D, 2 * FF), ((0, 2), (1, 16)), -0.2, 0.2)), 3.988004024235714e-11, 3.988004093624653e-10),
        "reduce_second": jnp.clip(jnp.exp(math.log(3.988004093624653e-10) - 2.3025851 * jax.random.uniform(key_of[17], (FF, D), jnp.float32) ** steps_of(key_of[17], (FF, D), ((0, 2), (1, 16)), -0.2, 0.2)), 3.988004024235714e-11, 3.988004093624653e-10),
        "mixer_gain_second": jnp.clip(jnp.exp(math.log(3.988004093624653e-10) - 2.3025851 * jax.random.uniform(key_of[18], (D,), jnp.float32) ** steps_of(key_of[18], (D,), ((0, 16),), -0.2, 0.2)), 3.988004024235714e-11, 3.988004093624653e-10),
        "expand_gain_second": jnp.clip(jnp.exp(math.log(3.988004093624653e-10) - 2.3025851 * jax.random.uniform(key_of[19], (D,), jnp.float32) ** steps_of(key_of[19], (D,), ((0, 16),), -0.2, 0.2)), 3.988004024235714e-11, 3.988004093624653e-10),
    }


norm_eps = 1e-05
rope_base = 160000.0
beta_one = 0.9
beta_two = 0.999
adam_eps = 1e-08
learn_rate = 0.01
decay_rate = 0.1
adam_step = 10
clip_limit = 1.0

def round_half(values):
    return lax.optimization_barrier(values.astype(jnp.bfloat16)).astype(jnp.float32)

def layer_norm(values):
    centre = values - lax.optimization_barrier(jnp.mean(values, axis=-1, keepdims=True))
    scaled = lax.rsqrt(lax.optimization_barrier(jnp.mean(centre * centre, axis=-1, keepdims=True)) + norm_eps)
    return (centre * scaled, scaled)

def norm_backward(grad_out, normed, scaled, gain_row):
    inner_grad = grad_out * gain_row
    first_mean = lax.optimization_barrier(jnp.mean(inner_grad, axis=-1, keepdims=True))
    second_mean = lax.optimization_barrier(jnp.mean(inner_grad * normed, axis=-1, keepdims=True))
    return scaled * (inner_grad - first_mean - normed * second_mean)

def rope_tables(positions, half_dim):
    frequency = rope_base ** (-jnp.arange(half_dim, dtype=jnp.float32) / half_dim)
    angles = positions[:, None] * frequency[None, :]
    return (jnp.cos(angles), jnp.sin(angles))

def rotate(values, cosine, sine_table):
    half_dim = values.shape[-1] // 2
    front_half = values[..., :half_dim]
    back_half = values[..., half_dim:]
    cos_part = cosine[:, None, :]
    sin_part = sine_table[:, None, :]
    return jnp.concatenate([front_half * cos_part - back_half * sin_part, back_half * cos_part + front_half * sin_part], axis=-1)

def gated(gate_part, upper_part):
    return jax.nn.gelu(gate_part, approximate=False) * upper_part

def sequence_pass(x_block, dy_block, joint_bf, mixer_bf, expand_bf, shrink_bf, gain_one, gain_two, cosine, sine_table):
    seq_len = x_block.shape[0]
    split_shape = (seq_len, HEADS, HEAD_DIM)
    score_scale = 1.0 / math.sqrt(HEAD_DIM)
    inputs = x_block.astype(jnp.float32)
    normed_one, scaled_one = layer_norm(inputs)
    hidden_one = (normed_one * gain_one).astype(jnp.bfloat16)
    projected = jnp.dot(hidden_one, joint_bf, preferred_element_type=jnp.float32)
    queries = round_half(rotate(projected[:, :D].reshape(split_shape), cosine, sine_table))
    keys_rot = round_half(rotate(projected[:, D:2 * D].reshape(split_shape), cosine, sine_table))
    values_bf = round_half(projected[:, 2 * D:].reshape(split_shape))
    scores = jnp.einsum('qhd,khd->hqk', queries, keys_rot) * score_scale
    row_max = lax.optimization_barrier(jnp.max(scores, axis=-1, keepdims=True))
    log_total = row_max + jnp.log(lax.optimization_barrier(jnp.sum(jnp.exp(scores - row_max), axis=-1, keepdims=True)))
    probs_now = jnp.exp(scores - log_total)
    probs_half = round_half(probs_now)
    mixed_out = jnp.einsum('hqk,khd->qhd', probs_half, values_bf).reshape(seq_len, D).astype(jnp.bfloat16)
    resid_one = inputs + jnp.dot(mixed_out, mixer_bf, preferred_element_type=jnp.float32)
    normed_two, scaled_two = layer_norm(resid_one)
    hidden_two = (normed_two * gain_two).astype(jnp.bfloat16)
    expanded = jnp.dot(hidden_two, expand_bf, preferred_element_type=jnp.float32)
    gate_part = expanded[:, :FF]
    upper_part = expanded[:, FF:]
    gated_bf = gated(gate_part, upper_part).astype(jnp.bfloat16)
    output = (resid_one + jnp.dot(gated_bf, shrink_bf, preferred_element_type=jnp.float32)).astype(jnp.bfloat16)
    grad_out = dy_block.astype(jnp.float32)
    shrink_grad = jnp.dot(gated_bf.T, dy_block, preferred_element_type=jnp.float32)
    grad_gated = jnp.dot(dy_block, shrink_bf.T, preferred_element_type=jnp.float32)
    _, pullback = jax.vjp(gated, gate_part, upper_part)
    grad_gate, grad_upper = pullback(grad_gated)
    grad_expanded = jnp.concatenate([grad_gate, grad_upper], axis=1).astype(jnp.bfloat16)
    expand_grad = jnp.dot(hidden_two.T, grad_expanded, preferred_element_type=jnp.float32)
    grad_hidden_two = jnp.dot(grad_expanded, expand_bf.T, preferred_element_type=jnp.float32)
    gain_two_grad = lax.optimization_barrier(jnp.sum(grad_hidden_two * normed_two, axis=0))
    grad_resid = grad_out + norm_backward(grad_hidden_two, normed_two, scaled_two, gain_two)
    grad_resid_bf = grad_resid.astype(jnp.bfloat16)
    mixer_grad = jnp.dot(mixed_out.T, grad_resid_bf, preferred_element_type=jnp.float32)
    grad_mixed = round_half(jnp.dot(grad_resid_bf, mixer_bf.T, preferred_element_type=jnp.float32)).reshape(split_shape)
    row_delta = lax.optimization_barrier(jnp.sum(grad_mixed * mixed_out.reshape(split_shape).astype(jnp.float32), axis=-1))
    grad_probs = jnp.einsum('qhd,khd->hqk', grad_mixed, values_bf)
    grad_scores = round_half(probs_now * (grad_probs - row_delta.T[:, :, None]))
    grad_values = jnp.einsum('hqk,qhd->khd', probs_half, grad_mixed)
    grad_queries = jnp.einsum('hqk,khd->qhd', grad_scores, keys_rot) * score_scale
    grad_keys = jnp.einsum('hqk,qhd->khd', grad_scores, queries) * score_scale
    grad_projected = jnp.concatenate([rotate(grad_queries, cosine, -sine_table).reshape(seq_len, D), rotate(grad_keys, cosine, -sine_table).reshape(seq_len, D), grad_values.reshape(seq_len, D)], axis=1).astype(jnp.bfloat16)
    joint_grad = jnp.dot(hidden_one.T, grad_projected, preferred_element_type=jnp.float32)
    grad_hidden_one = jnp.dot(grad_projected, joint_bf.T, preferred_element_type=jnp.float32)
    gain_one_grad = lax.optimization_barrier(jnp.sum(grad_hidden_one * normed_one, axis=0))
    input_grad = grad_resid + norm_backward(grad_hidden_one, normed_one, scaled_one, gain_one)
    return (output, input_grad, (joint_grad, mixer_grad, expand_grad, shrink_grad, gain_one_grad, gain_two_grad))

def adam_update(master, grad_item, first_old, second_old, clip_factor, decay_weight):
    clipped = clip_factor * grad_item
    first_new = beta_one * first_old + (1.0 - beta_one) * clipped
    second_new = beta_two * second_old + (1.0 - beta_two) * clipped * clipped
    update = first_new / (1.0 - beta_one ** adam_step) / (jnp.sqrt(second_new / (1.0 - beta_two ** adam_step)) + adam_eps)
    return (master - learn_rate * (update + decay_weight * master), first_new, second_new)

def reference(hidden_in, out_grad, joint_weight, mixer_weight, expand_weight, reduce_weight, mixer_gain, expand_gain, joint_first, mixer_first, expand_first, reduce_first, mixer_gain_first, expand_gain_first, joint_second, mixer_second, expand_second, reduce_second, mixer_gain_second, expand_gain_second):
    joint_bf = joint_weight.astype(jnp.bfloat16)
    mixer_bf = mixer_weight.astype(jnp.bfloat16)
    expand_bf = expand_weight.astype(jnp.bfloat16)
    shrink_bf = reduce_weight.astype(jnp.bfloat16)
    gain_one = round_half(mixer_gain)
    gain_two = round_half(expand_gain)
    positions = jnp.arange(SEQ, dtype=jnp.float32)
    cosine, sine_table = rope_tables(positions, HEAD_DIM // 2)
    x_seqs = hidden_in.reshape(N_DP, SEQ, D)
    dy_seqs = out_grad.reshape(N_DP, SEQ, D)
    masters = (joint_weight, mixer_weight, expand_weight, reduce_weight, mixer_gain, expand_gain)
    zero_grads = tuple((jnp.zeros(master.shape, jnp.float32) for master in masters))

    def step_fn(totals, blocks):
        output, in_grad, grads = sequence_pass(blocks[0], blocks[1], joint_bf, mixer_bf, expand_bf, shrink_bf, gain_one, gain_two, cosine, sine_table)
        return (tuple((total_part + grad_part for total_part, grad_part in zip(totals, grads))), (output, in_grad))
    totals, (outputs, in_grads) = lax.scan(step_fn, zero_grads, (x_seqs, dy_seqs))
    norm_total = sum((jnp.sum(grad_item * grad_item) for grad_item in totals))
    clip_factor = jnp.minimum(1.0, clip_limit / (jnp.sqrt(norm_total) + 1e-06))
    firsts = (joint_first, mixer_first, expand_first, reduce_first, mixer_gain_first, expand_gain_first)
    seconds = (joint_second, mixer_second, expand_second, reduce_second, mixer_gain_second, expand_gain_second)
    decays = (decay_rate, decay_rate, decay_rate, decay_rate, 0.0, 0.0)
    results = [adam_update(masters[index], totals[index], firsts[index], seconds[index], clip_factor, decays[index]) for index in range(6)]
    return (outputs.reshape(TOKENS, D), in_grads.reshape(TOKENS, D), totals[0], totals[1], totals[2], totals[3], totals[4], totals[5], results[0][0], results[1][0], results[2][0], results[3][0], results[4][0], results[5][0], results[0][1], results[1][1], results[2][1], results[3][1], results[4][1], results[5][1], results[0][2], results[1][2], results[2][2], results[3][2], results[4][2], results[5][2])
```

```python
import math

import jax
import jax.numpy as jnp
from jax import lax
from jax.experimental import pallas as pl
from jax.experimental.pallas import tpu as pltpu
from jax.sharding import PartitionSpec as P

HEADS = 12


norm_eps = 1e-05
rope_base = 160000.0
beta_one = 0.9
beta_two = 0.999
adam_eps = 1e-08
learn_rate = 0.01
decay_rate = 0.1
adam_step = 10
clip_limit = 1.0
key_block = 512


def layer_norm(values):
    centre = values - jnp.mean(values, axis=-1, keepdims=True)
    scaled = lax.rsqrt(jnp.mean(centre * centre, axis=-1, keepdims=True) + norm_eps)
    return (centre * scaled, scaled)


def norm_backward(grad_out, normed, scaled, gain_row):
    inner_grad = grad_out * gain_row
    first_mean = jnp.mean(inner_grad, axis=-1, keepdims=True)
    second_mean = jnp.mean(inner_grad * normed, axis=-1, keepdims=True)
    return scaled * (inner_grad - first_mean - normed * second_mean)


def rope_tables(positions, half_dim):
    frequency = rope_base ** (-jnp.arange(half_dim, dtype=jnp.float32) / half_dim)
    angles = positions[:, None] * frequency[None, :]
    return (jnp.cos(angles), jnp.sin(angles))


def rotate(values, cosine, sine_table):
    half_dim = values.shape[-1] // 2
    front_half = values[..., :half_dim]
    back_half = values[..., half_dim:]
    cos_part = cosine[:, None, :]
    sin_part = sine_table[:, None, :]
    return jnp.concatenate(
        [
            front_half * cos_part - back_half * sin_part,
            back_half * cos_part + front_half * sin_part,
        ],
        axis=-1,
    )


def gated(gate_part, upper_part):
    return jax.nn.gelu(gate_part, approximate=False) * upper_part


def adam_update(master, grad_item, first_old, second_old, clip_factor, decay_weight):
    clipped = clip_factor * grad_item
    first_new = beta_one * first_old + (1.0 - beta_one) * clipped
    second_new = beta_two * second_old + (1.0 - beta_two) * clipped * clipped
    update = (
        first_new
        / (1.0 - beta_one**adam_step)
        / (jnp.sqrt(second_new / (1.0 - beta_two**adam_step)) + adam_eps)
    )
    return (master - learn_rate * (update + decay_weight * master), first_new, second_new)


def generic_body(
    hidden_in,
    out_grad,
    joint_weight,
    mixer_weight,
    expand_weight,
    reduce_weight,
    mixer_gain,
    expand_gain,
    joint_first,
    mixer_first,
    expand_first,
    reduce_first,
    mixer_gain_first,
    expand_gain_first,
    joint_second,
    mixer_second,
    expand_second,
    reduce_second,
    mixer_gain_second,
    expand_gain_second,
):
    columns = (
        lax.all_gather(joint_weight.astype(jnp.bfloat16), "dp", axis=1, tiled=True),
        lax.all_gather(mixer_weight.astype(jnp.bfloat16), "dp", axis=1, tiled=True),
        lax.all_gather(expand_weight.astype(jnp.bfloat16), "dp", axis=1, tiled=True),
        lax.all_gather(reduce_weight.astype(jnp.bfloat16), "dp", axis=1, tiled=True),
        lax.all_gather(mixer_gain.astype(jnp.bfloat16), "dp", axis=0, tiled=True),
        lax.all_gather(expand_gain.astype(jnp.bfloat16), "dp", axis=0, tiled=True),
    )
    joint_bf, mixer_bf, expand_bf, shrink_bf = (
        lax.all_gather(columns[0], "group", axis=0, tiled=True),
        lax.all_gather(columns[1], "group", axis=0, tiled=True),
        lax.all_gather(columns[2], "group", axis=0, tiled=True),
        lax.all_gather(columns[3], "group", axis=0, tiled=True),
    )
    gain_one = columns[4].astype(jnp.float32)
    gain_two = columns[5].astype(jnp.float32)
    model_width = joint_bf.shape[0]
    hidden_units = shrink_bf.shape[0]
    head_size = model_width // HEADS
    tok_count = hidden_in.shape[0]
    groups = lax.axis_size("group")
    split_shape = (tok_count, HEADS, head_size)
    score_scale = 1.0 / math.sqrt(head_size)
    positions = (
        lax.axis_index("group") * tok_count + jnp.arange(tok_count, dtype=jnp.int32)
    ).astype(jnp.float32)
    cosine, sine_table = rope_tables(positions, head_size // 2)
    inputs = hidden_in.astype(jnp.float32)
    normed_one, scaled_one = layer_norm(inputs)
    hidden_one = (normed_one * gain_one).astype(jnp.bfloat16)
    projected = jnp.dot(hidden_one, joint_bf, preferred_element_type=jnp.float32)
    queries = rotate(projected[:, :model_width].reshape(split_shape), cosine, sine_table).astype(
        jnp.bfloat16
    )
    keys_rot = rotate(
        projected[:, model_width : 2 * model_width].reshape(split_shape), cosine, sine_table
    ).astype(jnp.bfloat16)
    values_bf = projected[:, 2 * model_width :].astype(jnp.bfloat16)
    keys_flat = keys_rot.reshape(tok_count, model_width)
    start_state = (
        jnp.full((HEADS, tok_count), -jnp.inf, jnp.float32),
        jnp.zeros((HEADS, tok_count), jnp.float32),
        jnp.zeros(split_shape, jnp.float32),
    )
    carried = start_state
    pieces = (
        lax.all_gather(keys_flat, "group", axis=0, tiled=True),
        lax.all_gather(values_bf, "group", axis=0, tiled=True),
    )
    key_count = pieces[0].shape[0]
    step_rows = math.gcd(key_count, key_block)
    for begin in range(0, key_count, step_rows):
        attend_key_rows = pieces[0][begin : begin + step_rows]
        attend_run_max, attend_run_total, attend_run_acc = carried
        attend_key_count = attend_key_rows.shape[0]
        attend_key_part = attend_key_rows.reshape(attend_key_count, HEADS, head_size)
        attend_value_part = pieces[1][begin : begin + step_rows].reshape(
            attend_key_count, HEADS, head_size
        )
        attend_scores = (
            jnp.einsum("qhd,khd->hqk", queries, attend_key_part, preferred_element_type=jnp.float32)
            * score_scale
        )
        new_max = jnp.maximum(attend_run_max, jnp.max(attend_scores, axis=-1))
        factor = jnp.exp(attend_run_max - new_max)
        attend_probs_now = jnp.exp(attend_scores - new_max[:, :, None])
        new_total = attend_run_total * factor + jnp.sum(attend_probs_now, axis=-1)
        weighted = jnp.einsum(
            "hqk,khd->qhd",
            attend_probs_now.astype(jnp.bfloat16),
            attend_value_part,
            preferred_element_type=jnp.float32,
        )
        carried = (new_max, new_total, attend_run_acc * factor.T[:, :, None] + weighted)
    run_max, run_total, run_acc = carried
    log_total = run_max + jnp.log(run_total)
    mixed_out = (
        (run_acc / run_total.T[:, :, None]).reshape(tok_count, model_width).astype(jnp.bfloat16)
    )
    resid_one = inputs + jnp.dot(mixed_out, mixer_bf, preferred_element_type=jnp.float32)
    normed_two, scaled_two = layer_norm(resid_one)
    hidden_two = (normed_two * gain_two).astype(jnp.bfloat16)
    expanded = jnp.dot(hidden_two, expand_bf, preferred_element_type=jnp.float32)
    gate_part = expanded[:, :hidden_units]
    upper_part = expanded[:, hidden_units:]
    gated_bf = gated(gate_part, upper_part).astype(jnp.bfloat16)
    block_output = (
        resid_one + jnp.dot(gated_bf, shrink_bf, preferred_element_type=jnp.float32)
    ).astype(jnp.bfloat16)
    grad_out = out_grad.astype(jnp.float32)
    shrink_grad = jnp.dot(gated_bf.T, out_grad, preferred_element_type=jnp.float32)
    grad_gated = jnp.dot(out_grad, shrink_bf.T, preferred_element_type=jnp.float32)
    _, pullback = jax.vjp(gated, gate_part, upper_part)
    grad_gate, grad_upper = pullback(grad_gated)
    grad_expanded = jnp.concatenate([grad_gate, grad_upper], axis=1).astype(jnp.bfloat16)
    expand_grad = jnp.dot(hidden_two.T, grad_expanded, preferred_element_type=jnp.float32)
    grad_hidden_two = jnp.dot(grad_expanded, expand_bf.T, preferred_element_type=jnp.float32)
    gain_two_grad = jnp.sum(grad_hidden_two * normed_two, axis=0)
    grad_resid = grad_out + norm_backward(grad_hidden_two, normed_two, scaled_two, gain_two)
    grad_resid_bf = grad_resid.astype(jnp.bfloat16)
    mixer_grad = jnp.dot(mixed_out.T, grad_resid_bf, preferred_element_type=jnp.float32)
    grad_mixed = (
        jnp.dot(grad_resid_bf, mixer_bf.T, preferred_element_type=jnp.float32)
        .astype(jnp.bfloat16)
        .reshape(split_shape)
    )
    row_delta = jnp.sum(
        grad_mixed.astype(jnp.float32) * mixed_out.reshape(split_shape).astype(jnp.float32), axis=-1
    )
    back_state = (
        jnp.zeros(split_shape, jnp.float32),
        jnp.zeros((groups * tok_count, model_width), jnp.float32),
        jnp.zeros((groups * tok_count, model_width), jnp.float32),
    )
    carried = back_state
    pieces = (
        lax.all_gather(keys_flat, "group", axis=0, tiled=True),
        lax.all_gather(values_bf, "group", axis=0, tiled=True),
    )
    offset = jnp.int32(0)
    key_count = pieces[0].shape[0]
    step_rows = math.gcd(key_count, key_block)
    for begin in range(0, key_count, step_rows):
        key_rows = pieces[0][begin : begin + step_rows]
        back_offset = offset + begin
        back_query_grad, back_key_grads, back_value_grads = carried
        back_key_count = key_rows.shape[0]
        key_part = key_rows.reshape(back_key_count, HEADS, head_size)
        value_part = pieces[1][begin : begin + step_rows].reshape(back_key_count, HEADS, head_size)
        scores = (
            jnp.einsum("qhd,khd->hqk", queries, key_part, preferred_element_type=jnp.float32)
            * score_scale
        )
        probs_now = jnp.exp(scores - log_total[:, :, None])
        value_term = jnp.einsum(
            "hqk,qhd->khd",
            probs_now.astype(jnp.bfloat16),
            grad_mixed,
            preferred_element_type=jnp.float32,
        ).reshape(back_key_count, model_width)
        grad_probs = jnp.einsum(
            "qhd,khd->hqk", grad_mixed, value_part, preferred_element_type=jnp.float32
        )
        grad_scores = (probs_now * (grad_probs - row_delta.T[:, :, None])).astype(jnp.bfloat16)
        back_query_grad = (
            back_query_grad
            + jnp.einsum("hqk,khd->qhd", grad_scores, key_part, preferred_element_type=jnp.float32)
            * score_scale
        )
        key_term = (
            jnp.einsum("hqk,qhd->khd", grad_scores, queries, preferred_element_type=jnp.float32)
            * score_scale
        ).reshape(back_key_count, model_width)
        back_key_grads = lax.dynamic_update_slice_in_dim(
            back_key_grads,
            lax.dynamic_slice_in_dim(back_key_grads, back_offset, back_key_count, 0) + key_term,
            back_offset,
            0,
        )
        back_value_grads = lax.dynamic_update_slice_in_dim(
            back_value_grads,
            lax.dynamic_slice_in_dim(back_value_grads, back_offset, back_key_count, 0) + value_term,
            back_offset,
            0,
        )
        carried = (back_query_grad, back_key_grads, back_value_grads)
    query_grad, key_grads, value_grads = carried
    key_sum, value_sum = (
        lax.psum_scatter(key_grads, "group", scatter_dimension=0, tiled=True),
        lax.psum_scatter(value_grads, "group", scatter_dimension=0, tiled=True),
    )
    grad_projected = jnp.concatenate(
        [
            rotate(query_grad, cosine, -sine_table).reshape(tok_count, model_width),
            rotate(key_sum.reshape(split_shape), cosine, -sine_table).reshape(
                tok_count, model_width
            ),
            value_sum,
        ],
        axis=1,
    ).astype(jnp.bfloat16)
    joint_grad = jnp.dot(hidden_one.T, grad_projected, preferred_element_type=jnp.float32)
    grad_hidden_one = jnp.dot(grad_projected, joint_bf.T, preferred_element_type=jnp.float32)
    gain_one_grad = jnp.sum(grad_hidden_one * normed_one, axis=0)
    input_grad = grad_resid + norm_backward(grad_hidden_one, normed_one, scaled_one, gain_one)
    across = (
        lax.psum_scatter(joint_grad, "dp", scatter_dimension=1, tiled=True),
        lax.psum_scatter(mixer_grad, "dp", scatter_dimension=1, tiled=True),
        lax.psum_scatter(expand_grad, "dp", scatter_dimension=1, tiled=True),
        lax.psum_scatter(shrink_grad, "dp", scatter_dimension=1, tiled=True),
        lax.psum_scatter(gain_one_grad, "dp", scatter_dimension=0, tiled=True),
        lax.psum_scatter(gain_two_grad, "dp", scatter_dimension=0, tiled=True),
    )
    tiled_one = jnp.broadcast_to(across[4][None, :], (groups, across[4].shape[0]))
    tiled_two = jnp.broadcast_to(across[5][None, :], (groups, across[5].shape[0]))
    owned_grads = (
        lax.psum_scatter(across[0], "group", scatter_dimension=0, tiled=True),
        lax.psum_scatter(across[1], "group", scatter_dimension=0, tiled=True),
        lax.psum_scatter(across[2], "group", scatter_dimension=0, tiled=True),
        lax.psum_scatter(across[3], "group", scatter_dimension=0, tiled=True),
        lax.psum_scatter(tiled_one, "group", scatter_dimension=0, tiled=True),
        lax.psum_scatter(tiled_two, "group", scatter_dimension=0, tiled=True),
    )
    owned_list = [
        owned_grads[0],
        owned_grads[1],
        owned_grads[2],
        owned_grads[3],
        owned_grads[4].reshape(-1),
        owned_grads[5].reshape(-1),
    ]
    matrix_squares = sum((jnp.sum(grad_item * grad_item) for grad_item in owned_list[:4]))
    gain_squares = jnp.sum(owned_list[4] * owned_list[4]) + jnp.sum(owned_list[5] * owned_list[5])
    squares = matrix_squares + jnp.where(lax.axis_index("group") == 0, gain_squares, 0.0)
    norm_total = lax.psum(squares, ("dp", "group"))
    clip_factor = jnp.minimum(1.0, clip_limit / (jnp.sqrt(norm_total) + 1e-06))
    masters = (joint_weight, mixer_weight, expand_weight, reduce_weight, mixer_gain, expand_gain)
    firsts = (
        joint_first,
        mixer_first,
        expand_first,
        reduce_first,
        mixer_gain_first,
        expand_gain_first,
    )
    seconds = (
        joint_second,
        mixer_second,
        expand_second,
        reduce_second,
        mixer_gain_second,
        expand_gain_second,
    )
    decays = (decay_rate, decay_rate, decay_rate, decay_rate, 0.0, 0.0)
    results = [
        adam_update(
            masters[index],
            owned_list[index],
            firsts[index],
            seconds[index],
            clip_factor,
            decays[index],
        )
        for index in range(6)
    ]
    return (
        block_output,
        input_grad,
        owned_list[0],
        owned_list[1],
        owned_list[2],
        owned_list[3],
        owned_list[4],
        owned_list[5],
        results[0][0],
        results[1][0],
        results[2][0],
        results[3][0],
        results[4][0],
        results[5][0],
        results[0][1],
        results[1][1],
        results[2][1],
        results[3][1],
        results[4][1],
        results[5][1],
        results[0][2],
        results[1][2],
        results[2][2],
        results[3][2],
        results[4][2],
        results[5][2],
    )


bf16 = jnp.bfloat16
f32 = jnp.float32
vmem_bytes = 60 * 1024 * 1024


def nt_dot(lhs, rhs):
    return lax.dot_general(lhs, rhs, (((1,), (1,)), ((), ())), preferred_element_type=f32)


def nn_dot(lhs, rhs):
    return lax.dot_general(lhs, rhs, (((1,), (0,)), ((), ())), preferred_element_type=f32)


def kernel_call(kernel, outs, args, any_from=None, any_to=None, scratch=(), flops=0, name=None):
    vmem_spec = pl.BlockSpec(memory_space=pltpu.VMEM)
    any_spec = pl.BlockSpec(memory_space=pl.ANY)
    specs = [
        any_spec if any_from is not None and any_from <= index < any_to else vmem_spec
        for index in range(len(args))
    ]
    moved = sum(math.prod(a.shape) * a.dtype.itemsize for a in args)
    moved += sum(math.prod(shape) * jnp.dtype(kind).itemsize for shape, kind in outs)
    return pl.pallas_call(
        kernel,
        out_shape=[jax.ShapeDtypeStruct(shape, kind) for shape, kind in outs],
        in_specs=specs,
        out_specs=[vmem_spec for _ in outs],
        scratch_shapes=list(scratch),
        compiler_params=pltpu.CompilerParams(vmem_limit_bytes=vmem_bytes),
        cost_estimate=pl.CostEstimate(flops=flops, bytes_accessed=moved, transcendentals=0),
        name=name,
    )(*args)


class Plan:
    def __init__(self, n_dp, n_group):
        self.n_dp = n_dp
        self.n_z = n_dp // 4

    def place(self):
        dp = lax.axis_index("dp")
        return dp // 4, (dp // 2) % 2, dp % 2, lax.axis_index("group")

    def core(self, value):
        return lax.ppermute(value, "dp", [(i, i ^ 1) for i in range(self.n_dp)])

    def across(self, value):
        return lax.ppermute(value, "dp", [(i, i ^ 2) for i in range(self.n_dp)])

    def along(self, value, step):
        pairs = [(i, ((i // 4 + step) % self.n_z) * 4 + i % 4) for i in range(self.n_dp)]
        return lax.ppermute(value, "dp", pairs)

    def group(self, value):
        return lax.ppermute(value, "group", [(0, 1), (1, 0)])

    def gather(self, chunk):
        parts = [chunk] + [self.along(chunk, step) for step in range(1, self.n_z)]
        mine = jnp.stack(parts)
        half = self.n_z // 2
        from_x = self.across(mine)
        from_g = self.group(mine)
        first = self.group(from_x[:half])
        second = self.across(from_g[half:])
        near = [
            (mine, 0, 0, 0),
            (from_x, 0, 1, 0),
            (from_g, 0, 0, 1),
            (first, 0, 1, 1),
            (second, half, 1, 1),
        ]
        pieces = [(array, slot, dx, dg, 0) for array, slot, dx, dg in near]
        pieces += [(self.core(array), slot, dx, dg, 1) for array, slot, dx, dg in near]
        return pieces

    def copies(self, refs, layout, sections, sems):
        z, x, c, g = self.place()
        started = []
        for ref, (count, slot, dx, dg, dc) in zip(refs, layout):
            for index in range(count):
                source_z = lax.rem(z - (slot + index) + self.n_z, self.n_z)
                source_dp = (source_z * 2 + (x ^ dx)) * 2 + (c ^ dc)
                source_g = g ^ dg
                for row, rows, lanes, target in sections:
                    started.append(
                        pltpu.make_async_copy(
                            ref.at[index, row : row + rows, 0:lanes],
                            target(source_dp, source_g),
                            sems.at[len(started)],
                        )
                    )
        for copy in started:
            copy.start()
        return started

    def scatter(self, outputs):
        send_a, keep_a, send_b, keep_b = outputs
        got_a = self.across(send_a)
        got_b = self.group(send_b)
        next_a = (keep_a[:, 1].astype(f32) + got_a[:, 1].astype(f32)).astype(bf16)
        next_b = (keep_b[:, 1].astype(f32) + got_b[:, 1].astype(f32)).astype(bf16)
        more_a = self.group(next_a)
        more_b = self.across(next_b)
        total_a = keep_a[:, 0].astype(f32) + got_a[:, 0].astype(f32) + more_a.astype(f32)
        total_b = keep_b[:, 0].astype(f32) + got_b[:, 0].astype(f32) + more_b.astype(f32)
        total = jnp.concatenate([total_a, total_b], axis=1).astype(bf16)
        z = lax.axis_index("dp") // 4
        result = lax.dynamic_index_in_dim(total, z, 0, keepdims=False).astype(f32)
        for step in range(1, self.n_z):
            piece = lax.dynamic_index_in_dim(total, (z + step) % self.n_z, 0, keepdims=False)
            result = result + self.along(piece, step).astype(f32)
        return result


def swap_halves(tile, half):
    lanes = tile.shape[1]
    lane = lax.broadcasted_iota(jnp.int32, tile.shape, 1)
    front = lane % (2 * half) < half
    return jnp.where(front, pltpu.roll(tile, lanes - half, 1), pltpu.roll(tile, half, 1))


def head_masks(rows, head):
    lane = lax.broadcasted_iota(jnp.int32, (rows, 2 * head), 1)
    return (lane < head, lane >= head)


def fast_body(plan, *args):
    (
        hidden_in,
        out_grad,
        joint_weight,
        mixer_weight,
        expand_weight,
        reduce_weight,
        mixer_gain,
        expand_gain,
    ) = args[:8]
    firsts = args[8:14]
    seconds = args[14:20]
    n_dp, n_z = plan.n_dp, plan.n_z
    tok, width = hidden_in.shape
    lanes = joint_weight.shape[0]
    joint_rows = joint_weight.shape[1]
    mixer_rows = mixer_weight.shape[1]
    expand_rows = expand_weight.shape[1]
    reduce_rows = reduce_weight.shape[1]
    units = 2 * reduce_weight.shape[0]
    rest = reduce_weight.shape[0] - lanes
    gain_size = mixer_gain.shape[0]
    head = width // HEADS
    tiles = width // (2 * head)
    tile_w = 2 * head
    scale = 1.0 / math.sqrt(head)
    blocks = n_dp // 2
    dp_index = lax.axis_index("dp")

    gains = jnp.stack([mixer_gain, expand_gain]).astype(bf16)
    gain_rows = lax.dynamic_update_slice(
        jnp.zeros((2, width), bf16), gains, (0, dp_index * gain_size)
    ).reshape(2 * width // lanes, lanes)
    gain_rows = jnp.pad(gain_rows, ((0, 16 - gain_rows.shape[0]), (0, 0)))
    chunk_one = jnp.concatenate([joint_weight.T.astype(bf16), gain_rows])
    reduce_t = reduce_weight.T.astype(bf16)
    chunk_two = jnp.concatenate(
        [
            mixer_weight.T.astype(bf16),
            expand_weight.T.astype(bf16),
            reduce_t[:, :lanes],
            jnp.pad(reduce_t[:, lanes:], ((0, 0), (0, lanes - rest))),
        ]
    )
    pieces_one = plan.gather(chunk_one)
    pieces_two = plan.gather(chunk_two)
    layout_one = [(p[0].shape[0],) + p[1:] for p in pieces_one]
    layout_two = [(p[0].shape[0],) + p[1:] for p in pieces_two]
    arrays_one = [p[0] for p in pieces_one]
    arrays_two = [p[0] for p in pieces_two]
    n_pieces = len(pieces_one)
    shards = 2 * n_dp

    positions = (
        lax.axis_index("group") * tok + jnp.arange(tok, dtype=jnp.int32)
    ).astype(f32)
    half = head // 2
    cos_half, sin_half = rope_tables(positions, half)
    cos_tab = jnp.tile(cos_half, (1, 4))
    sin_tab = jnp.concatenate([-sin_half, sin_half, -sin_half, sin_half], axis=1)

    def rows_at(ref, rows):
        return lambda dp, g: ref.at[
            pl.ds(pl.multiple_of(dp * rows, 16), rows), pl.ds(pl.multiple_of(g * lanes, 128), lanes)
        ]

    def project_kernel(*refs):
        x_ref, cos_ref, sin_ref = refs[:3]
        piece_refs = refs[3 : 3 + n_pieces]
        h1_ref, q_ref, kv_ref, gain_ref, w_ref, g_ref, sems = refs[3 + n_pieces :]
        copies = plan.copies(
            piece_refs,
            layout_one,
            [
                (0, joint_rows, lanes, rows_at(w_ref, joint_rows)),
                (joint_rows, 16, lanes, lambda dp, g: g_ref.at[dp * 2 + g]),
            ],
            sems,
        )
        normed, _ = layer_norm(x_ref[...].astype(f32))
        for copy in copies:
            copy.wait()
        summed = 0.5 * jnp.sum(g_ref[...].astype(f32), axis=0)
        row_one = jnp.concatenate([summed[0:1], summed[1:2]], axis=1)
        row_two = jnp.concatenate([summed[2:3], summed[3:4]], axis=1)
        gain_ref[...] = jnp.concatenate(
            [jnp.broadcast_to(row_one, (8, width)), jnp.broadcast_to(row_two, (8, width))], axis=0
        )
        hidden = (normed * row_one).astype(bf16)
        h1_ref[...] = hidden
        wide = 2 * tile_w
        cosine = jnp.concatenate([cos_ref[...]] * 2, axis=1)
        sine = jnp.concatenate([sin_ref[...]] * 2, axis=1)
        for n in range(3 * width // wide):
            start = n * wide
            tile = nt_dot(hidden, w_ref[start : start + wide, :])
            if start < 2 * width:
                tile = tile * cosine + swap_halves(tile, half) * sine
            if start < width:
                q_ref[:, start : start + wide] = tile.astype(bf16)
            else:
                kv_ref[:, start - width : start - width + wide] = tile.astype(bf16)

    hidden_one, queries, kv_own, gain_full = kernel_call(
        project_kernel,
        [((tok, width), bf16), ((tok, width), bf16), ((tok, 2 * width), bf16), ((16, width), f32)],
        [hidden_in, cos_tab, sin_tab] + arrays_one,
        any_from=3,
        any_to=3 + n_pieces,
        scratch=[
            pltpu.VMEM((3 * width, width), bf16),
            pltpu.VMEM((shards, 16, lanes), bf16),
            pltpu.SemaphoreType.DMA((2 * shards,)),
        ],
        flops=6 * tok * width * width,
        name="project",
    )
    kv_got = plan.group(kv_own)
    queries_got = plan.group(queries)

    def attend_kernel(q_ref, kv_ref, kvg_ref, o_ref, lse_ref):
        masks = head_masks(tok, head)
        lane = lax.broadcasted_iota(jnp.int32, (tok, tile_w), 1)
        lse_all = jnp.zeros((tok, tile_w), f32)
        for t in range(tiles):
            at = slice(t * tile_w, (t + 1) * tile_w)
            av = slice(width + t * tile_w, width + (t + 1) * tile_w)
            keys = jnp.concatenate([kv_ref[:, at], kvg_ref[:, at]], axis=0)
            values = jnp.concatenate([kv_ref[:, av], kvg_ref[:, av]], axis=0)
            q_tile = q_ref[:, at]
            out = jnp.zeros((tok, tile_w), f32)
            for h in range(2):
                scores = nt_dot(jnp.where(masks[h], q_tile, jnp.zeros_like(q_tile)), keys) * scale
                top = jnp.max(scores, axis=1, keepdims=True)
                weights = jnp.exp(scores - top)
                total = jnp.sum(weights, axis=1, keepdims=True)
                probs = (weights * (1.0 / total)).astype(bf16)
                out = jnp.where(masks[h], nn_dot(probs, values), out)
                lse_all = jnp.where(lane == 16 + 2 * t + h, top + jnp.log(total), lse_all)
            o_ref[:, at] = out.astype(bf16)
        lse_ref[...] = lse_all

    mixed_out, lse = kernel_call(
        attend_kernel,
        [((tok, width), bf16), ((tok, tile_w), f32)],
        [queries, kv_own, kv_got],
        flops=8 * tok * tok * width,
        name="attend",
    )

    split_shapes = [
        ((blocks, rows, tok), bf16)
        for rows in (expand_rows, expand_rows, reduce_rows, reduce_rows, mixer_rows, mixer_rows)
    ]

    def middle_kernel(*refs):
        x_ref, o_ref, og_ref, gain_ref, lse_ref = refs[:5]
        piece_refs = refs[5 : 5 + n_pieces]
        (
            out_ref,
            h2_ref,
            z_ref,
            dy1_ref,
            pack_ref,
            gg_ref,
            e_mine,
            e_theirs,
            r_mine,
            r_theirs,
            m_mine,
            m_theirs,
            wm_ref,
            we_ref,
            ra_ref,
            rb_ref,
            wr_ref,
            du_ref,
            dut_ref,
            dyt_ref,
            ogt_ref,
            sems,
        ) = refs[5 + n_pieces :]
        row_a = mixer_rows + expand_rows
        row_b = row_a + reduce_rows
        copies = plan.copies(
            piece_refs,
            layout_two,
            [
                (0, mixer_rows, lanes, rows_at(wm_ref, mixer_rows)),
                (mixer_rows, expand_rows, lanes, rows_at(we_ref, expand_rows)),
                (row_a, reduce_rows, lanes, rows_at(ra_ref, reduce_rows)),
                (row_b, reduce_rows, lanes, rows_at(rb_ref, reduce_rows)),
            ],
            sems,
        )
        inputs = x_ref[...].astype(f32)
        grad_out = og_ref[...].astype(f32)
        ogt_ref[...] = grad_out.T.astype(bf16)
        gain_two = gain_ref[8:9, :]
        for copy in copies:
            copy.wait()
        for start in range(0, width, 2 * tile_w):
            at = slice(start, start + 2 * tile_w)
            wr_ref[at, :] = jnp.concatenate(
                [
                    ra_ref[at, :lanes],
                    rb_ref[at, :rest],
                    ra_ref[at, lanes:],
                    rb_ref[at, lanes : lanes + rest],
                ],
                axis=1,
            )
        resid = inputs + nt_dot(o_ref[...], wm_ref[...])
        normed, scaled = layer_norm(resid)
        hidden = (normed * gain_two).astype(bf16)
        h2_ref[...] = hidden
        wide = lanes
        for n in range(units // wide):
            at = slice(n * wide, (n + 1) * wide)
            bt = slice(units + n * wide, units + (n + 1) * wide)
            gate = nt_dot(hidden, we_ref[at, :])
            upper = nt_dot(hidden, we_ref[bt, :])
            cdf = 0.5 * (1.0 + lax.erf(gate * (1.0 / math.sqrt(2.0))))
            gelu = gate * cdf
            z_ref[:, at] = (gelu * upper).astype(bf16)
            dz = nn_dot(og_ref[...], wr_ref[:, at])
            slope = cdf + gate * jnp.exp(-0.5 * gate * gate) * (1.0 / math.sqrt(2.0 * math.pi))
            d_gate = dz * upper * slope
            d_upper = dz * gelu
            du_ref[:, at] = d_gate.astype(bf16)
            du_ref[:, bt] = d_upper.astype(bf16)
            dut_ref[at, :] = d_gate.T.astype(bf16)
            dut_ref[bt, :] = d_upper.T.astype(bf16)
        out_ref[...] = (resid + nt_dot(z_ref[...], wr_ref[...])).astype(bf16)
        dh2 = nn_dot(du_ref[...], we_ref[...])
        gg_ref[...] = jnp.broadcast_to(jnp.sum(dh2 * normed, axis=0, keepdims=True), (8, width))
        dy1 = grad_out + norm_backward(dh2, normed, scaled, gain_two)
        dy1_ref[...] = dy1
        dyb = dy1.astype(bf16)
        dyt_ref[...] = dy1.T.astype(bf16)
        d_mixed = nn_dot(dyb, wm_ref[...]).astype(bf16)
        pack_ref[:, :width] = d_mixed
        product = d_mixed.astype(f32) * o_ref[...].astype(f32)
        masks = head_masks(tok, head)
        lane = lax.broadcasted_iota(jnp.int32, (tok, tile_w), 1)
        aux = lse_ref[...]
        for t in range(tiles):
            part = product[:, t * tile_w : (t + 1) * tile_w]
            for h in range(2):
                delta = jnp.sum(jnp.where(masks[h], part, 0.0), axis=1, keepdims=True)
                aux = jnp.where(lane == 2 * t + h, delta, aux)
        high = aux.astype(bf16)
        pack_ref[:, width : width + tile_w] = high
        pack_ref[:, width + tile_w :] = (aux - high.astype(f32)).astype(bf16)
        _, _, c, _ = plan.place()
        for j in range(blocks):
            for rows, source, mine, theirs in (
                (expand_rows, dut_ref, e_mine, e_theirs),
                (reduce_rows, ogt_ref, r_mine, r_theirs),
                (mixer_rows, dyt_ref, m_mine, m_theirs),
            ):
                mine[j] = source[pl.ds(pl.multiple_of((2 * j + c) * rows, 16), rows), :]
                theirs[j] = source[pl.ds(pl.multiple_of((2 * j + 1 - c) * rows, 16), rows), :]

    (
        block_output,
        hidden_two,
        gated_bf,
        grad_resid,
        packed_own,
        gain_two_part,
        e_mine,
        e_theirs,
        r_mine,
        r_theirs,
        m_mine,
        m_theirs,
    ) = kernel_call(
        middle_kernel,
        [
            ((tok, width), bf16),
            ((tok, width), bf16),
            ((tok, units), bf16),
            ((tok, width), f32),
            ((tok, width + 2 * tile_w), bf16),
            ((8, width), f32),
        ]
        + split_shapes,
        [hidden_in, mixed_out, out_grad, gain_full, lse] + arrays_two,
        any_from=5,
        any_to=5 + n_pieces,
        scratch=[
            pltpu.VMEM((width, width), bf16),
            pltpu.VMEM((2 * units, width), bf16),
            pltpu.VMEM((width, width), bf16),
            pltpu.VMEM((width, width), bf16),
            pltpu.VMEM((width, units), bf16),
            pltpu.VMEM((tok, 2 * units), bf16),
            pltpu.VMEM((2 * units, tok), bf16),
            pltpu.VMEM((width, tok), bf16),
            pltpu.VMEM((width, tok), bf16),
            pltpu.SemaphoreType.DMA((4 * shards,)),
        ],
        flops=4 * tok * (width * width + 3 * width * units),
        name="middle",
    )
    packed_got = plan.group(packed_own)

    def gradient_terms(sections, gain_sum, name):
        count = len(sections)
        widths = [section[2].shape[1] for section in sections]
        heights = [
            section[0].shape[1] * (1 if w == width else 2) for section, w in zip(sections, widths)
        ]
        extra = 0 if gain_sum is None else 16
        total = sum(heights) + extra
        cut = total // 2 // 16 * 16

        def kernel(*refs):
            ins = refs[: 4 * count]
            gain_ref = refs[4 * count] if extra else None
            outs = refs[4 * count + (1 if extra else 0) :]
            send_a, keep_a, send_b, keep_b, block = outs
            _, x, _, g = plan.place()
            if extra:
                for side in range(2):
                    block[side, total - 16 :, :] = gain_ref[...].astype(bf16)
            acts = [
                jnp.concatenate([ins[4 * i + 2][...], ins[4 * i + 3][...]], axis=0)
                for i in range(count)
            ]
            for step in (1, 0):
                for z in range(n_z):
                    j = z * 2 + (x ^ step)
                    row = 0
                    for i in range(count):
                        left = jnp.concatenate([ins[4 * i][j], ins[4 * i + 1][j]], axis=1)
                        value = nn_dot(left, acts[i]).astype(bf16)
                        rows = left.shape[0]
                        if widths[i] == width:
                            block[0, row : row + rows, :] = value[:, :lanes]
                            block[1, row : row + rows, :] = value[:, lanes:]
                            row += rows
                        else:
                            side_w = widths[i] // 2
                            pad = jnp.zeros((rows, lanes - rest), bf16)
                            for side in range(2):
                                base = side * side_w
                                block[side, row : row + rows, :] = value[:, base : base + lanes]
                                block[side, row + rows : row + 2 * rows, :] = jnp.concatenate(
                                    [value[:, base + lanes : base + side_w], pad], axis=1
                                )
                            row += 2 * rows
                    target = send_a if step else keep_a
                    target[z, 0] = block[g, :cut, :]
                    target[z, 1] = block[1 - g, :cut, :]
                    send_b[z, step] = block[1 - g, cut:, :]
                    keep_b[z, step] = block[g, cut:, :]

        shape_a = ((n_z, 2, cut, lanes), bf16)
        shape_b = ((n_z, 2, total - cut, lanes), bf16)
        args = [array for section in sections for array in section]
        if extra:
            args.append(gain_sum)
        return kernel_call(
            kernel,
            [shape_a, shape_a, shape_b, shape_b],
            args,
            scratch=[pltpu.VMEM((2, total, lanes), bf16)],
            flops=4 * tok * blocks * 2 * total * lanes,
            name=name,
        )

    early = gradient_terms(
        [
            (e_mine, plan.core(e_theirs), hidden_two, plan.core(hidden_two)),
            (r_mine, plan.core(r_theirs), gated_bf, plan.core(gated_bf)),
        ],
        None,
        "early_terms",
    )
    early_sum = plan.scatter(early)

    def attend_back_kernel(
        q_ref, qg_ref, kv_ref, kvg_ref, p_ref, pg_ref, cos_ref, sin_ref, d_ref, mine, theirs, dt_ref
    ):
        masks = head_masks(tok, head)
        masks_f = [mask.astype(f32) for mask in masks]
        ends = (width, width + tile_w)
        aux_own = p_ref[:, ends[0] : ends[1]].astype(f32) + p_ref[:, ends[1] :].astype(f32)
        aux_got = pg_ref[:, ends[0] : ends[1]].astype(f32) + pg_ref[:, ends[1] :].astype(f32)
        aux_t = jnp.concatenate([aux_own.T, aux_got.T], axis=1)
        cosine = cos_ref[...]
        sine = sin_ref[...]
        for t in range(tiles):
            at = slice(t * tile_w, (t + 1) * tile_w)
            av = slice(width + t * tile_w, width + (t + 1) * tile_w)
            keys = jnp.concatenate([kv_ref[:, at], kvg_ref[:, at]], axis=0)
            values = jnp.concatenate([kv_ref[:, av], kvg_ref[:, av]], axis=0)
            all_q = jnp.concatenate([q_ref[:, at], qg_ref[:, at]], axis=0)
            all_d = jnp.concatenate([p_ref[:, at], pg_ref[:, at]], axis=0)
            grads = [jnp.zeros((tok, tile_w), f32) for _ in range(3)]
            zero = jnp.zeros((tok, tile_w), bf16)
            for h in range(2):
                n = 2 * t + h
                scores = nt_dot(jnp.where(masks[h], q_ref[:, at], zero), keys) * scale
                probs = jnp.exp(scores - aux_own[:, 16 + n : 17 + n])
                d_probs = nt_dot(jnp.where(masks[h], p_ref[:, at], zero), values)
                d_scores = (probs * (d_probs - aux_own[:, n : n + 1])).astype(bf16)
                grads[0] += masks_f[h] * nn_dot(d_scores, keys)
                scores_t = nt_dot(jnp.where(masks[h], kv_ref[:, at], zero), all_q) * scale
                probs_t = jnp.exp(scores_t - aux_t[16 + n : 17 + n, :])
                d_probs_t = nt_dot(jnp.where(masks[h], kv_ref[:, av], zero), all_d)
                d_scores_t = (probs_t * (d_probs_t - aux_t[n : n + 1, :])).astype(bf16)
                grads[1] += masks_f[h] * nn_dot(d_scores_t, all_q)
                grads[2] += masks_f[h] * nn_dot(probs_t.astype(bf16), all_d)
            for i in range(3):
                value = grads[i]
                if i < 2:
                    value = value * scale
                    value = value * cosine - swap_halves(value, half) * sine
                to = slice(i * width + t * tile_w, i * width + (t + 1) * tile_w)
                d_ref[:, to] = value.astype(bf16)
                dt_ref[to, :] = value.T.astype(bf16)
        _, _, c, _ = plan.place()
        for j in range(blocks):
            first = pl.multiple_of((2 * j + c) * joint_rows, 16)
            other = pl.multiple_of((2 * j + 1 - c) * joint_rows, 16)
            mine[j] = dt_ref[pl.ds(first, joint_rows), :]
            theirs[j] = dt_ref[pl.ds(other, joint_rows), :]

    grad_projected, j_mine, j_theirs = kernel_call(
        attend_back_kernel,
        [
            ((tok, 3 * width), bf16),
            ((blocks, joint_rows, tok), bf16),
            ((blocks, joint_rows, tok), bf16),
        ],
        [queries, queries_got, kv_own, kv_got, packed_own, packed_got, cos_tab, sin_tab],
        scratch=[pltpu.VMEM((3 * width, tok), bf16)],
        flops=28 * tok * tok * width,
        name="attend_back",
    )

    def input_kernel(*refs):
        x_ref, dy1_ref, d_ref, gain_ref = refs[:4]
        piece_refs = refs[4 : 4 + n_pieces]
        out_ref, gg_ref, w_ref, sems = refs[4 + n_pieces :]
        copies = plan.copies(
            piece_refs, layout_one, [(0, joint_rows, lanes, rows_at(w_ref, joint_rows))], sems
        )
        normed, scaled = layer_norm(x_ref[...].astype(f32))
        for copy in copies:
            copy.wait()
        dh1 = nn_dot(d_ref[...], w_ref[...])
        gg_ref[...] = jnp.broadcast_to(jnp.sum(dh1 * normed, axis=0, keepdims=True), (8, width))
        out_ref[...] = dy1_ref[...] + norm_backward(dh1, normed, scaled, gain_ref[0:1, :])

    input_grad, gain_one_part = kernel_call(
        input_kernel,
        [((tok, width), f32), ((8, width), f32)],
        [hidden_in, grad_resid, grad_projected, gain_full] + arrays_one,
        any_from=4,
        any_to=4 + n_pieces,
        scratch=[
            pltpu.VMEM((3 * width, width), bf16),
            pltpu.SemaphoreType.DMA((shards,)),
        ],
        flops=6 * tok * width * width,
        name="input_grad",
    )
    gain_part = jnp.concatenate([gain_one_part[:1], gain_two_part[:1]]).reshape(
        2 * width // lanes, lanes
    )
    gain_part = jnp.pad(gain_part, ((0, 16 - gain_part.shape[0]), (0, 0)))
    gain_sum = gain_part + plan.core(gain_part)

    late = gradient_terms(
        [
            (m_mine, plan.core(m_theirs), mixed_out, plan.core(mixed_out)),
            (j_mine, plan.core(j_theirs), hidden_one, plan.core(hidden_one)),
        ],
        gain_sum,
        "late_terms",
    )
    late_sum = plan.scatter(late)

    expand_t = early_sum[:expand_rows]
    reduce_tt = jnp.concatenate(
        [
            early_sum[expand_rows : expand_rows + reduce_rows],
            early_sum[expand_rows + reduce_rows :, :rest],
        ],
        axis=1,
    )
    mixer_t = late_sum[:mixer_rows]
    joint_t = late_sum[mixer_rows : mixer_rows + joint_rows]
    gain_all = late_sum[mixer_rows + joint_rows :][: 2 * width // lanes].reshape(2, width)
    gain_mine = lax.dynamic_slice(gain_all, (0, dp_index * gain_size), (2, gain_size))
    owned = [joint_t.T, mixer_t.T, expand_t.T, reduce_tt.T, gain_mine[0], gain_mine[1]]
    squares = sum(jnp.sum(item * item) for item in owned[:4])
    squares = squares + jnp.sum(gain_all * gain_all) / (2 * n_dp)
    total = jnp.full((8, 128), squares, f32)
    total = total + plan.core(total)
    total = total + plan.across(total)
    total = total + plan.group(total)
    step = 1
    while step < n_z:
        pairs = [(i, ((i // 4) ^ step) * 4 + i % 4) for i in range(n_dp)]
        total = total + lax.ppermute(total, "dp", pairs)
        step *= 2
    clip_factor = jnp.minimum(1.0, clip_limit / (jnp.sqrt(total[0, 0]) + 1e-06))
    decays = (decay_rate, decay_rate, decay_rate, decay_rate, 0.0, 0.0)
    results = [
        adam_update(args[2 + i], owned[i], firsts[i], seconds[i], clip_factor, decays[i])
        for i in range(6)
    ]
    return (
        (block_output, input_grad)
        + tuple(owned)
        + tuple(r[0] for r in results)
        + tuple(r[1] for r in results)
        + tuple(r[2] for r in results)
    )


def fast_shapes(n_dp, n_group, args):
    tokens, width = args[0].shape
    units = args[5].shape[0]
    if n_group != 2 or n_dp % 8 or (n_dp // 4) & (n_dp // 4 - 1):
        return False
    tok = tokens // (n_dp * n_group)
    lanes = width // n_group
    rest = units // n_group - lanes
    rows = [args[i].shape[1] // n_dp for i in (2, 3, 4, 5)]
    return (
        tok == 128
        and width == 64 * HEADS
        and HEADS % 4 == 0
        and HEADS <= 16
        and lanes % 128 == 0
        and 0 < rest <= lanes
        and units % lanes == 0
        and all(r % 16 == 0 for r in rows)
    )


def pick_body(n_dp, n_group, args):
    if fast_shapes(n_dp, n_group, args):
        plan = Plan(n_dp, n_group)
        return lambda *parts: fast_body(plan, *parts)
    return generic_body


def solution(mesh):
    return lambda *args: jax.shard_map(
        pick_body(mesh.shape["dp"], mesh.shape["group"], args),
        mesh=mesh,
        in_specs=(
            P(("dp", "group"), None),
            P(("dp", "group"), None),
            P("group", "dp"),
            P("group", "dp"),
            P("group", "dp"),
            P("group", "dp"),
            P("dp"),
            P("dp"),
            P("group", "dp"),
            P("group", "dp"),
            P("group", "dp"),
            P("group", "dp"),
            P("dp"),
            P("dp"),
            P("group", "dp"),
            P("group", "dp"),
            P("group", "dp"),
            P("group", "dp"),
            P("dp"),
            P("dp"),
        ),
        out_specs=(
            P(("dp", "group"), None),
            P(("dp", "group"), None),
            P("group", "dp"),
            P("group", "dp"),
            P("group", "dp"),
            P("group", "dp"),
            P("dp"),
            P("dp"),
            P("group", "dp"),
            P("group", "dp"),
            P("group", "dp"),
            P("group", "dp"),
            P("dp"),
            P("dp"),
            P("group", "dp"),
            P("group", "dp"),
            P("group", "dp"),
            P("group", "dp"),
            P("dp"),
            P("dp"),
            P("group", "dp"),
            P("group", "dp"),
            P("group", "dp"),
            P("group", "dp"),
            P("dp"),
            P("dp"),
        ),
        check_vma=False,
    )(*args)
```
